256 devices in a mesh: energy: 128 (over y_hi, z, x, core), mom: 2 (over y_lo).
Axes of the slice: x: 4, y: 4 (y_hi: 2, y_lo: 2; y = y_hi * 2 + y_lo), z: 8, core: 2. Of those that a mesh axis runs over, the one named last changes fastest.
Arguments:
- hamiltonian: float32 [2, 2, 2, 128, 128], P('mom'), may hold values from -0.125 to 0.125
- hopping: float32 [2, 2, 128, 128], P('mom'), may hold values from -0.21875 to 0.21875
- self_energy: float32 [2, 128, 2, 2, 128, 128], P('mom', 'energy'), may hold values from -0.078125 to 0.078125
- screened: float32 [2, 128, 2, 2, 128, 128], P('mom', 'energy'), may hold values from -24 to 24
- energy_map: int32 [128], P('energy'), may hold values from 0 to 127, each once
Outputs:
- new_sigma: float32 [2, 128, 2, 2, 128, 128], P('mom', 'energy')
- polar: float32 [2, 2, 128, 32768], P('mom', None, None, 'energy')
The draws below stay inside these ranges and needn't reach their ends.
Inputs may be any that keep to these rules, and one draw needn't show every extreme that they name: energy_map is a permutation: every grid point 0 to 127 is held by exactly one slot.
All inputs are finite; a program needn't handle non-finite values.
Results may differ from the reference program's by a relative error of at most 0.0001.
Values sent between devices are 32-bit elements; how exact they have to be, the bound alone decides.
No kernel may reach another device: no remote copies, remote signals or barrier semaphores. Data moves between devices by JAX's collectives and lax.ppermute only.
A program may use at most 128 MiB of HBM per device.

```python
import jax
import jax.numpy as jnp
from jax import lax

B = 128
NB = 2
NE = 128
NK = 2
N_ENERGY = 128


def levels(own_key, shape, cuts, least, top_value):
    def one(position, parts):
        steps = jax.random.uniform(jax.random.fold_in(jax.random.fold_in(own_key, 6), position), (parts,), jnp.float32, least / len(cuts), top_value / len(cuts))
        return jnp.repeat(jnp.exp(steps), shape[position] // parts).reshape((-1,) + (1,) * (len(shape) - position - 1))

    level = one(*cuts[0])
    for cut in cuts[1:]:
        level = level * one(*cut)
    return level


def centred(rng, extent, width, reach, split=(), kind=jnp.bfloat16):
    factor_of = levels(rng, extent, split, -0.22, 0.18) if split else 1.0
    result = jax.random.normal(rng, extent, jnp.float32) * width * factor_of
    return jnp.minimum(jnp.maximum(result, -reach), reach).astype(kind)


def setup_inputs(seed: int = 0) -> dict:
    arg_keys = jax.random.split(jax.random.key(seed), 6)
    return {
        "hamiltonian": centred(arg_keys[0], (NK, NB, 2, B, B), (16 * B) ** -0.5, 0.125, ((0, 2),), jnp.float32),
        "hopping": centred(arg_keys[1], (NK, 2, B, B), (6 * B) ** -0.5, 0.21875, ((0, 2),), jnp.float32),
        "self_energy": centred(arg_keys[2], (NK, NE, 2, NB, B, B), (44 * B) ** -0.5, 0.078125, ((0, 2), (1, 128)), jnp.float32),
        "screened": centred(arg_keys[3], (NK, NE, 2, NB, B, B), 4.0, 24.0, ((0, 2), (1, 128)), jnp.float32),
        "energy_map": jax.random.permutation(arg_keys[4], NE).astype(jnp.int32),
    }


energy_floor = -2.0
energy_span = 4.0
broadening = 1.0
chemical = 0.0
thermal = 0.25


def occupation(energy):
    return 1.0 / (1.0 + jnp.exp((energy - chemical) / thermal))


def cmatmul(left_pair, right_pair):
    def product(left_factor, right_factor):
        return jnp.dot(left_factor, right_factor, preferred_element_type=jnp.float32, precision=lax.Precision.HIGHEST)
    return (product(left_pair[0], right_pair[0]) - product(left_pair[1], right_pair[1]),
            product(left_pair[0], right_pair[1]) + product(left_pair[1], right_pair[0]))


def approx_inverse(mat_pair):
    mat_re, mat_im = mat_pair
    dimension = mat_re.shape[-1]
    diag_re = jnp.diagonal(mat_re)
    diag_im = jnp.diagonal(mat_im)
    magnitude = diag_re * diag_re + diag_im * diag_im
    recip_re = diag_re / magnitude
    recip_im = -diag_im / magnitude
    outer_re = recip_re[:, None] * recip_re[None, :] - recip_im[:, None] * recip_im[None, :]
    outer_im = recip_re[:, None] * recip_im[None, :] + recip_im[:, None] * recip_re[None, :]
    identity = jnp.eye(dimension, dtype=mat_re.dtype)
    first_re = 2.0 * identity * recip_re[None, :] - (outer_re * mat_re - outer_im * mat_im)
    first_im = 2.0 * identity * recip_im[None, :] - (outer_re * mat_im + outer_im * mat_re)
    applied = cmatmul((mat_re, mat_im), (first_re, first_im))
    second = cmatmul((first_re, first_im), applied)
    return (2.0 * first_re - second[0], 2.0 * first_im - second[1])


def spectral_blocks(hermitian, coupling, sigma_pair, energy):
    blocks = hermitian[0].shape[0]
    dimension = hermitian[0].shape[-1]
    identity = jnp.eye(dimension, dtype=hermitian[0].dtype)
    adjoint = (coupling[0].T, -coupling[1].T)

    def shifted(block_id):
        return (energy * identity - hermitian[0][block_id] - sigma_pair[0][block_id],
                broadening * identity - hermitian[1][block_id] - sigma_pair[1][block_id])

    left_green = [approx_inverse(shifted(0))]
    for block_id in range(1, blocks):
        coupled = cmatmul(cmatmul(adjoint, left_green[-1]), coupling)
        shifted_block = shifted(block_id)
        left_green.append(approx_inverse((shifted_block[0] - coupled[0], shifted_block[1] - coupled[1])))
    full_green = [left_green[-1]]
    for block_id in range(blocks - 2, -1, -1):
        local_green = left_green[block_id]
        outgoing = cmatmul(local_green, coupling)
        incoming = cmatmul(adjoint, local_green)
        middle = cmatmul(cmatmul(outgoing, full_green[0]), incoming)
        full_green.insert(0, (local_green[0] + middle[0], local_green[1] + middle[1]))
    spec_re = jnp.stack([-(green[1] + green[1].T) for green in full_green])
    spec_im = jnp.stack([green[0] - green[0].T for green in full_green])
    return jnp.stack([spec_re, spec_im])


def reference(hamiltonian, hopping, self_energy, screened, energy_map):
    moments = hamiltonian.shape[0]
    slot_count = energy_map.shape[0]
    blocks = hamiltonian.shape[1]
    block_order = hamiltonian.shape[-1]
    elements = blocks * block_order * block_order
    spacing = energy_span / slot_count
    energies = energy_floor + spacing * energy_map.astype(jnp.float32)
    spectra_list = []
    for moment_id in range(moments):
        raw_re = hamiltonian[moment_id, :, 0]
        raw_im = hamiltonian[moment_id, :, 1]
        hermitian = (0.5 * (raw_re + jnp.swapaxes(raw_re, 1, 2)), 0.5 * (raw_im - jnp.swapaxes(raw_im, 1, 2)))
        coupling = (hopping[moment_id, 0], hopping[moment_id, 1])

        def solve_slot(packed, hermitian=hermitian, coupling=coupling):
            sigma_slot, energy = packed
            return spectral_blocks(hermitian, coupling, (sigma_slot[0], sigma_slot[1]), energy)

        spectra_list.append(lax.map(solve_slot, (self_energy[moment_id], energies)))
    spectra = jnp.stack(spectra_list)
    grid_order = jnp.argsort(energy_map).astype(jnp.int32)
    grid_spec = spectra[:, grid_order].reshape(moments, slot_count, 2, elements)
    grid_inter = screened[:, grid_order].reshape(moments, slot_count, 2, elements)
    grid_energy = energy_floor + spacing * jnp.arange(slot_count, dtype=jnp.int32).astype(jnp.float32)
    occupied = occupation(grid_energy)[None, :, None]
    pieces = N_ENERGY
    piece_width = elements // pieces
    length = 2 * slot_count

    def one_piece(piece_id):
        column_start = piece_id * piece_width
        spec_piece = lax.dynamic_slice_in_dim(grid_spec, column_start, piece_width, 3)
        inter_piece = lax.dynamic_slice_in_dim(grid_inter, column_start, piece_width, 3)
        complex_spec = lax.complex(spec_piece[:, :, 0], spec_piece[:, :, 1])
        lesser = occupied * complex_spec
        greater = (1.0 - occupied) * complex_spec
        interaction = lax.complex(inter_piece[:, :, 0], inter_piece[:, :, 1])
        lesser_hat = jnp.fft.fft(lesser, n=length, axis=1)
        greater_hat = jnp.fft.fft(greater, n=length, axis=1)
        inter_hat = jnp.fft.fft(interaction, n=length, axis=1)
        polar_list = []
        sigma_list = []
        for moment_id in range(moments):
            summed = greater_hat[0] * jnp.conj(lesser_hat[(0 - moment_id) % moments])
            for other_id in range(1, moments):
                summed = summed + greater_hat[other_id] * jnp.conj(lesser_hat[(other_id - moment_id) % moments])
            correlated = jnp.fft.ifft(summed, axis=0)[:slot_count]
            polar_list.append(jnp.stack([spacing * correlated.imag, -spacing * correlated.real]))
            folded = lesser_hat[moment_id % moments] * inter_hat[0]
            for other_id in range(1, moments):
                folded = folded + lesser_hat[(moment_id - other_id) % moments] * inter_hat[other_id]
            convolved = jnp.fft.ifft(folded, axis=0)[:slot_count]
            sigma_list.append(jnp.stack([-spacing * convolved.real, -spacing * convolved.imag], axis=1))
        return jnp.stack(polar_list), jnp.stack(sigma_list)

    polar_pieces, sigma_pieces = lax.map(one_piece, jnp.arange(pieces, dtype=jnp.int32))
    polar = jnp.moveaxis(polar_pieces, 0, 3).reshape(moments, 2, slot_count, elements)
    sigma_grid = jnp.moveaxis(sigma_pieces, 0, 3).reshape(moments, slot_count, 2, elements)
    new_sigma = sigma_grid[:, energy_map].reshape(moments, slot_count, 2, blocks, block_order, block_order)
    return new_sigma, polar
```

```python
import math

import jax
import jax.numpy as jnp
from jax import lax
from jax.sharding import PartitionSpec as P

energy_floor = -2.0
energy_span = 4.0
broadening = 1.0
chemical = 0.0
thermal = 0.25


def from_partner(array, axis, apart):
    return lax.ppermute(array, axis, [(i, i ^ 1 << apart) for i in range(lax.axis_size(axis))])


def occupation(energy):
    return 1.0 / (1.0 + jnp.exp((energy - chemical) / thermal))


def cmatmul(left_pair, right_pair):

    def product(left_factor, right_factor):
        return jnp.dot(
            left_factor,
            right_factor,
            preferred_element_type=jnp.float32,
            precision=lax.Precision.HIGHEST,
        )

    return (
        product(left_pair[0], right_pair[0]) - product(left_pair[1], right_pair[1]),
        product(left_pair[0], right_pair[1]) + product(left_pair[1], right_pair[0]),
    )


def approx_inverse(mat_pair):
    mat_re, mat_im = mat_pair
    dimension = mat_re.shape[-1]
    diag_re = jnp.diagonal(mat_re)
    diag_im = jnp.diagonal(mat_im)
    magnitude = diag_re * diag_re + diag_im * diag_im
    recip_re = diag_re / magnitude
    recip_im = -diag_im / magnitude
    outer_re = recip_re[:, None] * recip_re[None, :] - recip_im[:, None] * recip_im[None, :]
    outer_im = recip_re[:, None] * recip_im[None, :] + recip_im[:, None] * recip_re[None, :]
    identity = jnp.eye(dimension, dtype=mat_re.dtype)
    first_re = 2.0 * identity * recip_re[None, :] - (outer_re * mat_re - outer_im * mat_im)
    first_im = 2.0 * identity * recip_im[None, :] - (outer_re * mat_im + outer_im * mat_re)
    applied = cmatmul((mat_re, mat_im), (first_re, first_im))
    second = cmatmul((first_re, first_im), applied)
    return (2.0 * first_re - second[0], 2.0 * first_im - second[1])


def spectral_blocks(hermitian, coupling, sigma_pair, energy):
    blocks = hermitian[0].shape[0]
    dimension = hermitian[0].shape[-1]
    identity = jnp.eye(dimension, dtype=hermitian[0].dtype)
    adjoint = (coupling[0].T, -coupling[1].T)

    def shifted(block_id):
        return (
            energy * identity - hermitian[0][block_id] - sigma_pair[0][block_id],
            broadening * identity - hermitian[1][block_id] - sigma_pair[1][block_id],
        )

    left_green = [approx_inverse(shifted(0))]
    block_id = 1
    coupled = cmatmul(cmatmul(adjoint, left_green[-1]), coupling)
    shifted_block = shifted(block_id)
    left_green.append(
        approx_inverse((shifted_block[0] - coupled[0], shifted_block[1] - coupled[1]))
    )
    full_green = [left_green[-1]]
    block_id = 0
    local_green = left_green[block_id]
    outgoing = cmatmul(local_green, coupling)
    incoming = cmatmul(adjoint, local_green)
    middle = cmatmul(cmatmul(outgoing, full_green[0]), incoming)
    full_green.insert(0, (local_green[0] + middle[0], local_green[1] + middle[1]))
    spec_re = jnp.stack([-(green[1] + green[1].T) for green in full_green])
    spec_im = jnp.stack([green[0] - green[0].T for green in full_green])
    return jnp.stack([spec_re, spec_im])


def phase_table(row_index, column_index, length):
    wrapped = row_index[:, None] * column_index[None, :] % length
    return wrapped.astype(jnp.float32) * (2.0 * math.pi / length)


def select_pair(condition, first_pair, second_pair):
    return (
        jnp.where(condition, first_pair[0], second_pair[0]),
        jnp.where(condition, first_pair[1], second_pair[1]),
    )


def times_conj(left_pair, right_pair):
    return (
        left_pair[0] * right_pair[0] + left_pair[1] * right_pair[1],
        left_pair[1] * right_pair[0] - left_pair[0] * right_pair[1],
    )


def times_plain(left_pair, right_pair):
    return (
        left_pair[0] * right_pair[0] - left_pair[1] * right_pair[1],
        left_pair[0] * right_pair[1] + left_pair[1] * right_pair[0],
    )


def add_pairs(first_pair, second_pair):
    return (first_pair[0] + second_pair[0], first_pair[1] + second_pair[1])


def to_pieces(field):
    blocks, order = field.shape[1], field.shape[2]
    pieces = blocks * order // 2
    return jnp.swapaxes(field.reshape(2, pieces, 2, order), 0, 1).reshape(pieces, 4, order)


def from_pieces(chunks, blocks, order):
    pieces = chunks.shape[0]
    return jnp.swapaxes(chunks.reshape(pieces, 2, 2, order), 0, 1).reshape(2, blocks, order, order)


def exchange(chunks):
    return lax.all_to_all(chunks, "energy", split_axis=0, concat_axis=0, tiled=True)


def on_device(hamiltonian, hopping, self_energy, screened, energy_map):
    slot_count = lax.axis_size("energy")
    spacing = energy_span / slot_count
    blocks = hamiltonian.shape[1]
    block_order = hamiltonian.shape[-1]
    own_index = jnp.broadcast_to(energy_map[0].astype(jnp.float32), (slot_count, 1, 128))
    grid_index = exchange(own_index)[:, 0, 0].astype(jnp.int32)
    inter_own = exchange(to_pieces(screened[0, 0]))
    inter_other = from_partner(inter_own, "mom", 0)
    raw_re = hamiltonian[0, :, 0]
    raw_im = hamiltonian[0, :, 1]
    hermitian = (
        0.5 * (raw_re + jnp.swapaxes(raw_re, 1, 2)),
        0.5 * (raw_im - jnp.swapaxes(raw_im, 1, 2)),
    )
    coupling = (hopping[0, 0], hopping[0, 1])
    energy = energy_floor + spacing * energy_map[0].astype(jnp.float32)
    spectra = spectral_blocks(
        hermitian, coupling, (self_energy[0, 0, 0], self_energy[0, 0, 1]), energy
    )
    spec_own = exchange(to_pieces(spectra))
    spec_other = from_partner(spec_own, "mom", 0)
    length = 2 * slot_count
    frequency = jnp.arange(length, dtype=jnp.int32)
    forward_angle = phase_table(frequency, grid_index, length)
    forward = (jnp.cos(forward_angle), -jnp.sin(forward_angle))

    def pair(chunks):
        return (
            jnp.concatenate([chunks[:, 0], chunks[:, 1]], axis=1),
            jnp.concatenate([chunks[:, 2], chunks[:, 3]], axis=1),
        )

    def scaled(factor, field):
        return (factor * field[0], factor * field[1])

    def transform(field):
        return cmatmul(forward, field)

    grid_points = jnp.arange(slot_count, dtype=jnp.int32)
    polar_angle = phase_table(grid_points, frequency, length)
    inverse_grid = (jnp.cos(polar_angle) / length, jnp.sin(polar_angle) / length)
    slot_angle = phase_table(grid_index, frequency, length)
    inverse_slot = (jnp.cos(slot_angle) / length, jnp.sin(slot_angle) / length)
    first_is_own = lax.axis_index("mom") == 0
    occupied = occupation(energy_floor + spacing * grid_index.astype(jnp.float32))[:, None]
    own_pair = pair(spec_own)
    other_pair = pair(spec_other)
    lesser_a = transform(scaled(occupied, own_pair))
    lesser_b = transform(scaled(occupied, other_pair))
    greater_a = transform(scaled(1.0 - occupied, own_pair))
    greater_b = transform(scaled(1.0 - occupied, other_pair))
    inter_a = transform(pair(inter_own))
    inter_b = transform(pair(inter_other))
    greater_first = select_pair(first_is_own, greater_a, greater_b)
    greater_second = select_pair(first_is_own, greater_b, greater_a)
    lesser_first = select_pair(first_is_own, lesser_a, lesser_b)
    lesser_second = select_pair(first_is_own, lesser_b, lesser_a)
    polar_hat = add_pairs(times_conj(greater_first, lesser_a), times_conj(greater_second, lesser_b))
    sigma_hat = add_pairs(times_plain(lesser_first, inter_a), times_plain(lesser_second, inter_b))
    correlated = cmatmul(inverse_grid, polar_hat)
    polar = jnp.stack([spacing * correlated[1], -spacing * correlated[0]])
    convolved = cmatmul(inverse_slot, sigma_hat)
    half = block_order
    sigma_chunks = jnp.stack(
        [
            -spacing * convolved[0][:, :half],
            -spacing * convolved[0][:, half:],
            -spacing * convolved[1][:, :half],
            -spacing * convolved[1][:, half:],
        ],
        axis=1,
    )
    returned = exchange(sigma_chunks)
    new_sigma = from_pieces(returned, blocks, block_order)[None, None]
    return (new_sigma, polar[None])


def solution(mesh):
    return jax.shard_map(
        on_device,
        mesh=mesh,
        in_specs=(
            P("mom", None, None, None, None),
            P("mom", None, None, None),
            P("mom", "energy", None, None, None, None),
            P("mom", "energy", None, None, None, None),
            P("energy"),
        ),
        out_specs=(P("mom", "energy", None, None, None, None), P("mom", None, None, "energy")),
        check_vma=False,
    )
```

```python
import math

import jax
import jax.numpy as jnp
import numpy as np
from jax import lax
from jax.experimental import pallas as pl
from jax.experimental.pallas import tpu as pltpu
from jax.sharding import PartitionSpec as P

energy_floor = -2.0
energy_span = 4.0
broadening = 1.0
chemical = 0.0
thermal = 0.25

chunk_rows = 4
inter_rows = 5


def from_partner(array, axis):
    return lax.ppermute(array, axis, [(i, i ^ 1) for i in range(lax.axis_size(axis))])


def occupation(energy):
    return 1.0 / (1.0 + jnp.exp((energy - chemical) / thermal))


def halves(value):
    high = value.astype(jnp.bfloat16)
    return high, (value - high.astype(jnp.float32)).astype(jnp.bfloat16)


def dot(left, right):
    return jnp.dot(left, right, preferred_element_type=jnp.float32)


def dot3(left, right):
    return dot(left[0], right[0]) + (dot(left[0], right[1]) + dot(left[1], right[0]))


def left_form(pair):
    return halves(jnp.concatenate(pair, axis=1))


def right_form(pair):
    re, im = halves(pair[0]), halves(pair[1])
    return tuple(
        jnp.concatenate(
            [jnp.concatenate([re[n], im[n]], axis=1), jnp.concatenate([-im[n], re[n]], axis=1)],
            axis=0,
        )
        for n in range(2)
    )


def cproduct(left, right):
    result = dot3(left, right)
    order = result.shape[0]
    return result[:, :order], result[:, order:]


def approx_inverse(mat_re, mat_im, eye):
    def diagonal(values, axis):
        return jnp.sum(jnp.where(eye, values, 0.0), axis=axis, keepdims=True)

    def reciprocal(axis):
        diag_re, diag_im = diagonal(mat_re, axis), diagonal(mat_im, axis)
        magnitude = diag_re * diag_re + diag_im * diag_im
        return diag_re / magnitude, -diag_im / magnitude

    col_re, col_im = reciprocal(1)
    row_re, row_im = reciprocal(0)
    outer_re = col_re * row_re - col_im * row_im
    outer_im = col_re * row_im + col_im * row_re
    first_re = jnp.where(eye, 2.0 * row_re, 0.0) - (outer_re * mat_re - outer_im * mat_im)
    first_im = jnp.where(eye, 2.0 * row_im, 0.0) - (outer_re * mat_im + outer_im * mat_re)
    first = (first_re, first_im)
    applied = cproduct(left_form((mat_re, mat_im)), right_form(first))
    second = cproduct(left_form(first), right_form(applied))
    return 2.0 * first_re - second[0], 2.0 * first_im - second[1]


def pack_kernel(map_ref, screened_ref, out_ref):
    blocks, order = screened_ref.shape[3], screened_ref.shape[4]
    half = order // 2
    for part in range(2):
        for block in range(blocks):
            for low in range(2):
                start = block * half * inter_rows + part * 2 + low
                out_ref[pl.ds(start, half, stride=inter_rows), :] = screened_ref[
                    0, 0, part, block, pl.ds(low, half, stride=2), :
                ]
    pieces = blocks * half
    index = jnp.full((pieces, order), map_ref[0], jnp.int32).astype(jnp.float32)
    out_ref[pl.ds(4, pieces, stride=inter_rows), :] = index


def green_kernel(spacing, map_ref, ham_ref, hop_ref, self_ref, out_ref, spec_ref):
    order = ham_ref.shape[3]
    half = order // 2
    rows = lax.broadcasted_iota(jnp.int32, (order, order), 0)
    cols = lax.broadcasted_iota(jnp.int32, (order, order), 1)
    eye = rows == cols
    index = jnp.full((order, order), map_ref[0], jnp.int32).astype(jnp.float32)
    energy = energy_floor + spacing * index

    def shifted(block):
        raw_re, raw_im = ham_ref[0, block, 0], ham_ref[0, block, 1]
        herm_re = 0.5 * (raw_re + raw_re.T)
        herm_im = 0.5 * (raw_im - raw_im.T)
        return (
            jnp.where(eye, energy, 0.0) - herm_re - self_ref[0, 0, 0, block],
            jnp.where(eye, broadening, 0.0) - herm_im - self_ref[0, 0, 1, block],
        )

    hop = (hop_ref[0, 0], hop_ref[0, 1])
    adjoint = (hop[0].T, -hop[1].T)
    hop_right = right_form(hop)
    local = approx_inverse(*shifted(0), eye)
    incoming = cproduct(left_form(adjoint), right_form(local))
    outgoing = cproduct(left_form(local), hop_right)
    coupled = cproduct(left_form(incoming), hop_right)
    last = shifted(1)
    green = approx_inverse(last[0] - coupled[0], last[1] - coupled[1], eye)
    middle = cproduct(left_form(outgoing), right_form(green))
    middle = cproduct(left_form(middle), right_form(incoming))
    full = ((local[0] + middle[0], local[1] + middle[1]), green)
    for block in range(2):
        spec_ref[0] = -(full[block][1] + full[block][1].T)
        spec_ref[1] = full[block][0] - full[block][0].T
        for part in range(2):
            for low in range(2):
                start = block * half * chunk_rows + part * 2 + low
                out_ref[pl.ds(start, half, stride=chunk_rows), :] = spec_ref[
                    part, pl.ds(low, half, stride=2), :
                ]


def gather_field(ref, stride, scale=None):
    slots = ref.shape[0] // stride

    def part(row):
        values = ref[pl.ds(row, slots, stride=stride), :]
        return values if scale is None else scale * values

    return jnp.concatenate(
        [
            jnp.concatenate([part(0), part(1)], axis=1),
            jnp.concatenate([part(2), part(3)], axis=1),
        ],
        axis=0,
    )


def table_kernel(
    spacing, own_ref, other_ref, wave_ref, wave_t_ref, fwd_ref, inv_ref, hat_ref, occ_ref
):
    slots = occ_ref.shape[0]
    index = own_ref[pl.ds(4, slots, stride=inter_rows), :]
    occ_ref[...] = occupation(energy_floor + spacing * index)
    grid = lax.broadcasted_iota(jnp.int32, index.shape, 1).astype(jnp.float32)
    chosen = jnp.where(index == grid, 1.0, 0.0).astype(jnp.bfloat16)
    contract = (((1,), (1,)), ((), ()))
    for n in range(2):
        wave = [
            lax.dot_general(
                wave_ref[n, part], chosen, contract, preferred_element_type=jnp.float32
            ).astype(jnp.bfloat16)
            for part in range(2)
        ]
        fwd_ref[n] = jnp.concatenate(
            [
                jnp.concatenate([wave[0], -wave[1]], axis=1),
                jnp.concatenate([wave[1], wave[0]], axis=1),
            ],
            axis=0,
        )
        turned = [dot(chosen, wave_t_ref[n, part]).astype(jnp.bfloat16) for part in range(2)]
        inv_ref[n] = jnp.concatenate(
            [
                jnp.concatenate([turned[0], turned[1]], axis=1),
                jnp.concatenate([-turned[1], turned[0]], axis=1),
            ],
            axis=0,
        )
    forward = (fwd_ref[0], fwd_ref[1])
    hat_ref[0] = dot3(forward, halves(gather_field(own_ref, inter_rows)))
    hat_ref[1] = dot3(forward, halves(gather_field(other_ref, inter_rows)))


def sigma_kernel(
    spacing, mom_ref, own_ref, other_ref, occ_ref, fwd_ref, inv_ref, inter_ref, send_ref, hat_ref
):
    slots = occ_ref.shape[0]
    length = 2 * slots
    forward = (fwd_ref[0], fwd_ref[1])
    occupied = occ_ref[...]
    hat_ref[0] = dot3(forward, halves(gather_field(own_ref, chunk_rows, occupied)))
    hat_ref[1] = dot3(forward, halves(gather_field(other_ref, chunk_rows, occupied)))
    moment = mom_ref[0]
    sum_re = sum_im = 0.0
    for n, source in enumerate((moment, 1 - moment)):
        left_re, left_im = hat_ref[source, :length], hat_ref[source, length:]
        right_re, right_im = inter_ref[n, :length], inter_ref[n, length:]
        sum_re += left_re * right_re - left_im * right_im
        sum_im += left_re * right_im + left_im * right_re
    inverse = (inv_ref[0], inv_ref[1])
    result = dot3(inverse, halves(jnp.concatenate([sum_re, sum_im], axis=0)))
    result = result * (-spacing / length)
    for part in range(2):
        for low in range(2):
            send_ref[pl.ds(part * 2 + low, slots, stride=chunk_rows), :] = result[
                part * slots : (part + 1) * slots, low * 128 : (low + 1) * 128
            ]


def polar_kernel(
    spacing, mom_ref, own_ref, other_ref, occ_ref, fwd_ref, back_ref, hat_ref, out_ref, great_ref
):
    slots = occ_ref.shape[0]
    length = 2 * slots
    forward = (fwd_ref[0], fwd_ref[1])
    empty = 1.0 - occ_ref[...]
    great_ref[0] = dot3(forward, halves(gather_field(own_ref, chunk_rows, empty)))
    great_ref[1] = dot3(forward, halves(gather_field(other_ref, chunk_rows, empty)))
    moment = mom_ref[0]
    sum_re = sum_im = 0.0
    for n, source in enumerate((moment, 1 - moment)):
        left_re, left_im = great_ref[source, :length], great_ref[source, length:]
        right_re, right_im = hat_ref[n, :length], hat_ref[n, length:]
        sum_re += left_re * right_re + left_im * right_im
        sum_im += left_im * right_re - left_re * right_im
    back = (back_ref[0], back_ref[1])
    result = dot3(back, halves(jnp.concatenate([sum_re, sum_im], axis=0)))
    out_ref[0, 0] = result[slots:] * (spacing / length)
    out_ref[0, 1] = result[:slots] * (-spacing / length)


def unpack_kernel(recv_ref, out_ref):
    blocks, order = out_ref.shape[3], out_ref.shape[4]
    half = order // 2
    for part in range(2):
        for block in range(blocks):
            for low in range(2):
                start = block * half * chunk_rows + part * 2 + low
                out_ref[0, 0, part, block, pl.ds(low, half, stride=2), :] = recv_ref[
                    pl.ds(start, half, stride=chunk_rows), :
                ]


def call(kernel, outs, scalars, name, scratch=()):
    vmem = pl.BlockSpec(memory_space=pltpu.VMEM)
    smem = pl.BlockSpec(memory_space=pltpu.SMEM)

    def run(*operands):
        return pl.pallas_call(
            kernel,
            out_shape=outs,
            in_specs=[smem] * scalars + [vmem] * (len(operands) - scalars),
            out_specs=jax.tree.map(lambda _: vmem, outs),
            scratch_shapes=list(scratch),
            name=name,
        )(*operands)

    return run


def exchange(rows, count):
    chunks = rows.reshape(count, rows.shape[0] // count, rows.shape[1])
    moved = lax.all_to_all(chunks, "energy", split_axis=0, concat_axis=0, tiled=True)
    return moved.reshape(rows.shape)


def split_table(table):
    high = table.astype(np.float32).astype(jnp.bfloat16)
    low = (table - high.astype(np.float64)).astype(np.float32).astype(jnp.bfloat16)
    return np.stack([high, low])


def on_device(hamiltonian, hopping, self_energy, screened, energy_map):
    slots = lax.axis_size("energy")
    spacing = energy_span / slots
    length = 2 * slots
    order = hamiltonian.shape[-1]
    angle = (np.arange(length)[:, None] * np.arange(slots)[None, :] % length) * (
        2.0 * math.pi / length
    )
    wave = np.stack([np.cos(angle), -np.sin(angle)])
    wave_t = np.swapaxes(wave, 1, 2)
    back = np.block([[wave_t[0], wave_t[1]], [-wave_t[1], wave_t[0]]])
    wave, wave_t, back = (jnp.asarray(split_table(t)) for t in (wave, wave_t, back))

    def f32(*shape):
        return jax.ShapeDtypeStruct(shape, jnp.float32)

    def b16(*shape):
        return jax.ShapeDtypeStruct(shape, jnp.bfloat16)

    moment = lax.axis_index("mom").astype(jnp.int32).reshape(1)
    packed = call(pack_kernel, f32(slots * inter_rows, order), 1, "pack")(energy_map, screened)
    packed = packed.reshape(slots, 1, inter_rows * order)
    inter_own = lax.all_to_all(packed, "energy", split_axis=0, concat_axis=0, tiled=True)
    inter_own = inter_own.reshape(slots * inter_rows, order)
    inter_other = from_partner(inter_own, "mom")
    spectrum = call(
        lambda *refs: green_kernel(spacing, *refs),
        f32(slots * chunk_rows, order),
        1,
        "green",
        [pltpu.VMEM((2, order, order), jnp.float32)],
    )(energy_map, hamiltonian, hopping, self_energy)
    own = exchange(spectrum, slots)
    forward, inverse, inter_hat, occupied = call(
        lambda *refs: table_kernel(spacing, *refs),
        (
            b16(2, 2 * length, 2 * slots),
            b16(2, 2 * slots, 2 * length),
            f32(2, 2 * length, 2 * order),
            f32(slots, order),
        ),
        0,
        "tables",
    )(inter_own, inter_other, wave, wave_t)
    own, occupied = lax.optimization_barrier((own, occupied))
    other = from_partner(own, "mom")
    send, lesser_hat = call(
        lambda *refs: sigma_kernel(spacing, *refs),
        (f32(slots * chunk_rows, order), f32(2, 2 * length, 2 * order)),
        1,
        "sigma",
    )(moment, own, other, occupied, forward, inverse, inter_hat)
    returned = exchange(send, slots)
    polar = call(
        lambda *refs: polar_kernel(spacing, *refs),
        f32(1, 2, slots, 2 * order),
        1,
        "polar",
        [pltpu.VMEM((2, 2 * length, 2 * order), jnp.float32)],
    )(moment, own, other, occupied, forward, back, lesser_hat)
    new_sigma = call(unpack_kernel, f32(*screened.shape), 0, "unpack")(returned)
    return (new_sigma, polar)


def solution(mesh):
    return jax.shard_map(
        on_device,
        mesh=mesh,
        in_specs=(
            P("mom", None, None, None, None),
            P("mom", None, None, None),
            P("mom", "energy", None, None, None, None),
            P("mom", "energy", None, None, None, None),
            P("energy"),
        ),
        out_specs=(P("mom", "energy", None, None, None, None), P("mom", None, None, "energy")),
        check_vma=False,
    )
```

```python
import math

import jax
import jax.numpy as jnp
import numpy as np
from jax import lax
from jax.experimental import pallas as pl
from jax.experimental.pallas import tpu as pltpu
from jax.sharding import PartitionSpec as P

energy_floor = -2.0
energy_span = 4.0
broadening = 1.0
chemical = 0.0
thermal = 0.25

field_rows = 5


def from_partner(array, axis):
    return lax.ppermute(array, axis, [(i, i ^ 1) for i in range(lax.axis_size(axis))])


def occupation(energy):
    return 1.0 / (1.0 + jnp.exp((energy - chemical) / thermal))


def halves(value):
    high = value.astype(jnp.bfloat16)
    return high, (value - high.astype(jnp.float32)).astype(jnp.bfloat16)


def dot(left, right):
    return jnp.dot(left, right, preferred_element_type=jnp.float32)


def dot3(left, right):
    return dot(left[0], right[0]) + (dot(left[0], right[1]) + dot(left[1], right[0]))


def left_form(pair):
    return halves(jnp.concatenate(pair, axis=1))


def right_form(pair):
    re, im = halves(pair[0]), halves(pair[1])
    return tuple(
        jnp.concatenate(
            [jnp.concatenate([re[n], im[n]], axis=1), jnp.concatenate([-im[n], re[n]], axis=1)],
            axis=0,
        )
        for n in range(2)
    )


def cproduct(left, right):
    result = dot3(left, right)
    order = result.shape[0]
    return result[:, :order], result[:, order:]


def approx_inverse(mat_re, mat_im, eye):
    def diagonal(values, axis):
        return jnp.sum(jnp.where(eye, values, 0.0), axis=axis, keepdims=True)

    def reciprocal(axis):
        diag_re, diag_im = diagonal(mat_re, axis), diagonal(mat_im, axis)
        magnitude = diag_re * diag_re + diag_im * diag_im
        return diag_re / magnitude, -diag_im / magnitude

    col_re, col_im = reciprocal(1)
    row_re, row_im = reciprocal(0)
    outer_re = col_re * row_re - col_im * row_im
    outer_im = col_re * row_im + col_im * row_re
    first_re = jnp.where(eye, 2.0 * row_re, 0.0) - (outer_re * mat_re - outer_im * mat_im)
    first_im = jnp.where(eye, 2.0 * row_im, 0.0) - (outer_re * mat_im + outer_im * mat_re)
    first = (first_re, first_im)
    applied = cproduct(left_form((mat_re, mat_im)), right_form(first))
    second = cproduct(left_form(first), right_form(applied))
    return 2.0 * first_re - second[0], 2.0 * first_im - second[1]


def green_kernel(spacing, map_ref, ham_ref, hop_ref, self_ref, screened_ref, out_ref):
    order = ham_ref.shape[3]
    rows = lax.broadcasted_iota(jnp.int32, (order, order), 0)
    cols = lax.broadcasted_iota(jnp.int32, (order, order), 1)
    eye = rows == cols
    index = jnp.full((order, order), map_ref[0], jnp.int32).astype(jnp.float32)
    energy = energy_floor + spacing * index

    def put(block, row, values):
        start = block * order * field_rows + row
        out_ref[pl.ds(start, order, stride=field_rows), :] = values

    def shifted(block):
        raw_re, raw_im = ham_ref[0, block, 0], ham_ref[0, block, 1]
        herm_re = 0.5 * (raw_re + raw_re.T)
        herm_im = 0.5 * (raw_im - raw_im.T)
        return (
            jnp.where(eye, energy, 0.0) - herm_re - self_ref[0, 0, 0, block],
            jnp.where(eye, broadening, 0.0) - herm_im - self_ref[0, 0, 1, block],
        )

    for block in range(2):
        put(block, 2, screened_ref[0, 0, 0, block])
        put(block, 3, screened_ref[0, 0, 1, block])
        put(block, 4, index)
    hop = (hop_ref[0, 0], hop_ref[0, 1])
    adjoint = (hop[0].T, -hop[1].T)
    hop_right = right_form(hop)
    local = approx_inverse(*shifted(0), eye)
    incoming = cproduct(left_form(adjoint), right_form(local))
    outgoing = cproduct(left_form(local), hop_right)
    coupled = cproduct(left_form(incoming), hop_right)
    last = shifted(1)
    green = approx_inverse(last[0] - coupled[0], last[1] - coupled[1], eye)
    middle = cproduct(left_form(outgoing), right_form(green))
    middle = cproduct(left_form(middle), right_form(incoming))
    full = ((local[0] + middle[0], local[1] + middle[1]), green)
    for block in range(2):
        put(block, 0, -(full[block][1] + full[block][1].T))
        put(block, 1, full[block][0] - full[block][0].T)


def received(ref, row, scale=None):
    slots = ref.shape[0] // (2 * field_rows)

    def part(moment, n):
        start = moment * field_rows + row + n
        values = ref[pl.ds(start, slots, stride=2 * field_rows), :]
        return values if scale is None else scale * values

    return jnp.concatenate(
        [jnp.concatenate([part(0, n), part(1, n)], axis=1) for n in range(2)], axis=0
    )


def sigma_kernel(
    spacing, recv_ref, wave_ref, wave_t_ref, send_ref, fwd_ref, hat_ref, occ_ref
):
    slots, order = occ_ref.shape
    length = 2 * slots
    index = recv_ref[pl.ds(4, slots, stride=2 * field_rows), :]
    occupied = occupation(energy_floor + spacing * index)
    occ_ref[...] = occupied
    grid = lax.broadcasted_iota(jnp.int32, index.shape, 1).astype(jnp.float32)
    chosen = jnp.where(index == grid, 1.0, 0.0).astype(jnp.bfloat16)
    contract = (((1,), (1,)), ((), ()))
    forward, inverse = [], []
    for n in range(2):
        wave = [
            lax.dot_general(
                wave_ref[n, part], chosen, contract, preferred_element_type=jnp.float32
            ).astype(jnp.bfloat16)
            for part in range(2)
        ]
        forward.append(
            jnp.concatenate(
                [
                    jnp.concatenate([wave[0], -wave[1]], axis=1),
                    jnp.concatenate([wave[1], wave[0]], axis=1),
                ],
                axis=0,
            )
        )
        fwd_ref[n] = forward[n]
        turned = [dot(chosen, wave_t_ref[n, part]).astype(jnp.bfloat16) for part in range(2)]
        inverse.append(
            jnp.concatenate(
                [
                    jnp.concatenate([turned[0], turned[1]], axis=1),
                    jnp.concatenate([-turned[1], turned[0]], axis=1),
                ],
                axis=0,
            )
        )
    lesser = dot3(forward, halves(received(recv_ref, 0, occupied)))
    inter = dot3(forward, halves(received(recv_ref, 2)))
    hat_ref[...] = lesser

    def parts(hat, moment):
        return (
            hat[:length, moment * order : (moment + 1) * order],
            hat[length:, moment * order : (moment + 1) * order],
        )

    columns = []
    for moment in range(2):
        sum_re = sum_im = 0.0
        for transfer in range(2):
            left_re, left_im = parts(lesser, (moment - transfer) % 2)
            right_re, right_im = parts(inter, transfer)
            sum_re += left_re * right_re - left_im * right_im
            sum_im += left_re * right_im + left_im * right_re
        columns.append(jnp.concatenate([sum_re, sum_im], axis=0))
    result = dot3(inverse, halves(jnp.concatenate(columns, axis=1))) * (-spacing / length)
    for moment in range(2):
        for part in range(2):
            send_ref[pl.ds(moment * 2 + part, slots, stride=4), :] = result[
                part * slots : (part + 1) * slots, moment * order : (moment + 1) * order
            ]


def polar_kernel(
    spacing, mom_ref, recv_ref, occ_ref, fwd_ref, back_ref, hat_ref, keep_ref, give_ref, pol_ref
):
    slots, order = occ_ref.shape
    length = 2 * slots
    forward = (fwd_ref[0], fwd_ref[1])
    greater = dot3(forward, halves(received(recv_ref, 0, 1.0 - occ_ref[...])))

    def parts(hat, moment):
        return (
            hat[:length, moment * order : (moment + 1) * order],
            hat[length:, moment * order : (moment + 1) * order],
        )

    columns = []
    for transfer in range(2):
        sum_re = sum_im = 0.0
        for moment in range(2):
            left_re, left_im = parts(greater, moment)
            right_re, right_im = parts(hat_ref, (moment - transfer) % 2)
            sum_re += left_re * right_re + left_im * right_im
            sum_im += left_im * right_re - left_re * right_im
        columns.append(jnp.concatenate([sum_re, sum_im], axis=0))
    back = (back_ref[0], back_ref[1])
    result = dot3(back, halves(jnp.concatenate(columns, axis=1))) * (spacing / length)
    for transfer in range(2):
        chosen = result[:, transfer * order : (transfer + 1) * order]
        pol_ref[transfer, 0] = chosen[slots:]
        pol_ref[transfer, 1] = -chosen[:slots]
    keep_ref[...] = pol_ref[mom_ref[0]]
    give_ref[...] = pol_ref[1 - mom_ref[0]]


def finish_kernel(mom_ref, recv_ref, keep_ref, other_ref, sigma_ref, polar_ref):
    blocks, order = sigma_ref.shape[3], sigma_ref.shape[4]
    for part in range(2):
        for block in range(blocks):
            start = block * order * 2 + part
            sigma_ref[0, 0, part, block] = recv_ref[pl.ds(start, order, stride=2), :]
    first = mom_ref[0] == 0
    polar_ref[0, :, :, :order] = jnp.where(first, keep_ref[...], other_ref[...])
    polar_ref[0, :, :, order:] = jnp.where(first, other_ref[...], keep_ref[...])


def call(kernel, outs, scalars, name, scratch=()):
    vmem = pl.BlockSpec(memory_space=pltpu.VMEM)
    smem = pl.BlockSpec(memory_space=pltpu.SMEM)

    def run(*operands):
        return pl.pallas_call(
            kernel,
            out_shape=outs,
            in_specs=[smem] * scalars + [vmem] * (len(operands) - scalars),
            out_specs=jax.tree.map(lambda _: vmem, outs),
            scratch_shapes=list(scratch),
            name=name,
        )(*operands)

    return run


def exchange(chunks):
    return lax.all_to_all(chunks, ("energy", "mom"), split_axis=0, concat_axis=0, tiled=True)


def split_table(table):
    high = table.astype(np.float32).astype(jnp.bfloat16)
    low = (table - high.astype(np.float64)).astype(np.float32).astype(jnp.bfloat16)
    return np.stack([high, low])


def on_device(hamiltonian, hopping, self_energy, screened, energy_map):
    slots = lax.axis_size("energy")
    spacing = energy_span / slots
    length = 2 * slots
    order = hamiltonian.shape[-1]
    angle = (np.arange(length)[:, None] * np.arange(slots)[None, :] % length) * (
        2.0 * math.pi / length
    )
    wave = np.stack([np.cos(angle), -np.sin(angle)])
    wave_t = np.swapaxes(wave, 1, 2)
    back = np.block([[wave_t[0], wave_t[1]], [-wave_t[1], wave_t[0]]])
    wave, wave_t, back = (jnp.asarray(split_table(t)) for t in (wave, wave_t, back))

    def f32(*shape):
        return jax.ShapeDtypeStruct(shape, jnp.float32)

    def b16(*shape):
        return jax.ShapeDtypeStruct(shape, jnp.bfloat16)

    moment = lax.axis_index("mom").astype(jnp.int32).reshape(1)
    targets = 2 * slots
    fields = call(
        lambda *refs: green_kernel(spacing, *refs), f32(targets * field_rows, order), 1, "green"
    )(energy_map, hamiltonian, hopping, self_energy, screened)
    own = exchange(fields.reshape(targets, 1, field_rows * order)).reshape(fields.shape)
    send, forward, lesser_hat, occupied = call(
        lambda *refs: sigma_kernel(spacing, *refs),
        (
            f32(2 * targets, order),
            b16(2, 2 * length, 2 * slots),
            f32(2 * length, 2 * order),
            f32(slots, order),
        ),
        0,
        "sigma",
    )(own, wave, wave_t)
    returned = exchange(send.reshape(targets, 2, order)).reshape(send.shape)
    keep, give = call(
        lambda *refs: polar_kernel(spacing, *refs),
        (f32(2, slots, order), f32(2, slots, order)),
        1,
        "polar",
        [pltpu.VMEM((2, 2, slots, order), jnp.float32)],
    )(moment, own, occupied, forward, back, lesser_hat)
    other = from_partner(give, "mom")
    new_sigma, polar = call(
        finish_kernel, (f32(*screened.shape), f32(1, 2, slots, 2 * order)), 1, "finish"
    )(moment, returned, keep, other)
    return (new_sigma, polar)


def solution(mesh):
    return jax.shard_map(
        on_device,
        mesh=mesh,
        in_specs=(
            P("mom", None, None, None, None),
            P("mom", None, None, None),
            P("mom", "energy", None, None, None, None),
            P("mom", "energy", None, None, None, None),
            P("energy"),
        ),
        out_specs=(P("mom", "energy", None, None, None, None), P("mom", None, None, "energy")),
        check_vma=False,
    )
```

```python
import math

import jax
import jax.numpy as jnp
import numpy as np
from jax import lax
from jax.experimental import pallas as pl
from jax.experimental.pallas import tpu as pltpu
from jax.sharding import PartitionSpec as P

energy_floor = -2.0
energy_span = 4.0
broadening = 1.0
chemical = 0.0
thermal = 0.25

field_rows = 4


def from_partner(array, axis):
    return lax.ppermute(array, axis, [(i, i ^ 1) for i in range(lax.axis_size(axis))])


def occupation(energy):
    return 1.0 / (1.0 + jnp.exp((energy - chemical) / thermal))


def halves(value):
    high = value.astype(jnp.bfloat16)
    return high, (value - high.astype(jnp.float32)).astype(jnp.bfloat16)


def dot(left, right):
    return jnp.dot(left, right, preferred_element_type=jnp.float32)


def dot3(left, right):
    return dot(left[0], right[0]) + (dot(left[0], right[1]) + dot(left[1], right[0]))


def left_form(pair):
    return halves(jnp.concatenate(pair, axis=1))


def right_form(pair):
    re, im = halves(pair[0]), halves(pair[1])
    return tuple(
        jnp.concatenate(
            [jnp.concatenate([re[n], im[n]], axis=1), jnp.concatenate([-im[n], re[n]], axis=1)],
            axis=0,
        )
        for n in range(2)
    )


def cproduct(left, right):
    result = dot3(left, right)
    order = result.shape[0]
    return result[:, :order], result[:, order:]


def approx_inverse(mat_re, mat_im, eye):
    def diagonal(values, axis):
        return jnp.sum(jnp.where(eye, values, 0.0), axis=axis, keepdims=True)

    def reciprocal(axis):
        diag_re, diag_im = diagonal(mat_re, axis), diagonal(mat_im, axis)
        magnitude = diag_re * diag_re + diag_im * diag_im
        return diag_re / magnitude, -diag_im / magnitude

    col_re, col_im = reciprocal(1)
    row_re, row_im = reciprocal(0)
    outer_re = col_re * row_re - col_im * row_im
    outer_im = col_re * row_im + col_im * row_re
    first_re = jnp.where(eye, 2.0 * row_re, 0.0) - (outer_re * mat_re - outer_im * mat_im)
    first_im = jnp.where(eye, 2.0 * row_im, 0.0) - (outer_re * mat_im + outer_im * mat_re)
    first = (first_re, first_im)
    applied = cproduct(left_form((mat_re, mat_im)), right_form(first))
    second = cproduct(left_form(first), right_form(applied))
    return 2.0 * first_re - second[0], 2.0 * first_im - second[1]


def green_kernel(spacing, map_ref, ham_ref, hop_ref, self_ref, screened_ref, out_ref):
    order = ham_ref.shape[3]
    rows = lax.broadcasted_iota(jnp.int32, (order, order), 0)
    cols = lax.broadcasted_iota(jnp.int32, (order, order), 1)
    eye = rows == cols
    index = jnp.full((order, order), map_ref[0], jnp.int32).astype(jnp.float32)
    energy = energy_floor + spacing * index

    def put(block, row, values):
        start = block * order * field_rows + row
        out_ref[pl.ds(start, order, stride=field_rows), :] = values

    def shifted(block):
        raw_re, raw_im = ham_ref[0, block, 0], ham_ref[0, block, 1]
        herm_re = 0.5 * (raw_re + raw_re.T)
        herm_im = 0.5 * (raw_im - raw_im.T)
        return (
            jnp.where(eye, energy, 0.0) - herm_re - self_ref[0, 0, 0, block],
            jnp.where(eye, broadening, 0.0) - herm_im - self_ref[0, 0, 1, block],
        )

    for block in range(2):
        put(block, 2, screened_ref[0, 0, 0, block])
        put(block, 3, screened_ref[0, 0, 1, block])
    hop = (hop_ref[0, 0], hop_ref[0, 1])
    adjoint = (hop[0].T, -hop[1].T)
    hop_right = right_form(hop)
    local = approx_inverse(*shifted(0), eye)
    incoming = cproduct(left_form(adjoint), right_form(local))
    outgoing = cproduct(left_form(local), hop_right)
    coupled = cproduct(left_form(incoming), hop_right)
    last = shifted(1)
    green = approx_inverse(last[0] - coupled[0], last[1] - coupled[1], eye)
    middle = cproduct(left_form(outgoing), right_form(green))
    middle = cproduct(left_form(middle), right_form(incoming))
    full = ((local[0] + middle[0], local[1] + middle[1]), green)
    for block in range(2):
        put(block, 0, -(full[block][1] + full[block][1].T))
        put(block, 1, jnp.where(eye, index, full[block][0] - full[block][0].T))


def rows_of(ref, moment, row):
    slots = ref.shape[0] // (2 * field_rows)
    return ref[pl.ds(moment * field_rows + row, slots, stride=2 * field_rows), :]


def on_diagonal(column_ref, shape):
    return lax.broadcasted_iota(jnp.int32, shape, 1) == column_ref[0]


def spectrum(ref, diagonal, scale):
    real = [scale * rows_of(ref, moment, 0) for moment in range(2)]
    imag = [
        jnp.where(diagonal, 0.0, scale * rows_of(ref, moment, 1)) for moment in range(2)
    ]
    return jnp.concatenate(
        [jnp.concatenate(real, axis=1), jnp.concatenate(imag, axis=1)], axis=0
    )


def interaction(ref):
    return jnp.concatenate(
        [
            jnp.concatenate([rows_of(ref, moment, row) for moment in range(2)], axis=1)
            for row in (2, 3)
        ],
        axis=0,
    )


def sigma_kernel(
    spacing, column_ref, recv_ref, wave_ref, wave_t_ref, send_ref, fwd_ref, hat_ref, occ_ref
):
    slots, order = occ_ref.shape
    length = 2 * slots
    diagonal = on_diagonal(column_ref, occ_ref.shape)
    index = jnp.sum(
        jnp.where(diagonal, rows_of(recv_ref, 0, 1), 0.0), axis=1, keepdims=True
    )
    index = jnp.broadcast_to(index, occ_ref.shape)
    occupied = occupation(energy_floor + spacing * index)
    occ_ref[...] = occupied
    grid = lax.broadcasted_iota(jnp.int32, index.shape, 1).astype(jnp.float32)
    chosen = jnp.where(index == grid, 1.0, 0.0).astype(jnp.bfloat16)
    contract = (((1,), (1,)), ((), ()))
    forward, inverse = [], []
    for n in range(2):
        wave = [
            lax.dot_general(
                wave_ref[n, part], chosen, contract, preferred_element_type=jnp.float32
            ).astype(jnp.bfloat16)
            for part in range(2)
        ]
        forward.append(
            jnp.concatenate(
                [
                    jnp.concatenate([wave[0], -wave[1]], axis=1),
                    jnp.concatenate([wave[1], wave[0]], axis=1),
                ],
                axis=0,
            )
        )
        fwd_ref[n] = forward[n]
        turned = [dot(chosen, wave_t_ref[n, part]).astype(jnp.bfloat16) for part in range(2)]
        inverse.append(
            jnp.concatenate(
                [
                    jnp.concatenate([turned[0], turned[1]], axis=1),
                    jnp.concatenate([-turned[1], turned[0]], axis=1),
                ],
                axis=0,
            )
        )
    lesser = dot3(forward, halves(spectrum(recv_ref, diagonal, occupied)))
    inter = dot3(forward, halves(interaction(recv_ref)))
    hat_ref[...] = lesser

    def parts(hat, moment):
        return (
            hat[:length, moment * order : (moment + 1) * order],
            hat[length:, moment * order : (moment + 1) * order],
        )

    columns = []
    for moment in range(2):
        sum_re = sum_im = 0.0
        for transfer in range(2):
            left_re, left_im = parts(lesser, (moment - transfer) % 2)
            right_re, right_im = parts(inter, transfer)
            sum_re += left_re * right_re - left_im * right_im
            sum_im += left_re * right_im + left_im * right_re
        columns.append(jnp.concatenate([sum_re, sum_im], axis=0))
    result = dot3(inverse, halves(jnp.concatenate(columns, axis=1))) * (-spacing / length)
    for moment in range(2):
        for part in range(2):
            send_ref[pl.ds(moment * 2 + part, slots, stride=4), :] = result[
                part * slots : (part + 1) * slots, moment * order : (moment + 1) * order
            ]


def polar_kernel(
    spacing,
    mom_ref,
    column_ref,
    recv_ref,
    occ_ref,
    fwd_ref,
    back_ref,
    hat_ref,
    keep_ref,
    give_ref,
    pol_ref,
):
    slots, order = occ_ref.shape
    length = 2 * slots
    forward = (fwd_ref[0], fwd_ref[1])
    diagonal = on_diagonal(column_ref, occ_ref.shape)
    greater = dot3(forward, halves(spectrum(recv_ref, diagonal, 1.0 - occ_ref[...])))

    def parts(hat, moment):
        return (
            hat[:length, moment * order : (moment + 1) * order],
            hat[length:, moment * order : (moment + 1) * order],
        )

    columns = []
    for transfer in range(2):
        sum_re = sum_im = 0.0
        for moment in range(2):
            left_re, left_im = parts(greater, moment)
            right_re, right_im = parts(hat_ref, (moment - transfer) % 2)
            sum_re += left_re * right_re + left_im * right_im
            sum_im += left_im * right_re - left_re * right_im
        columns.append(jnp.concatenate([sum_re, sum_im], axis=0))
    back = (back_ref[0], back_ref[1])
    result = dot3(back, halves(jnp.concatenate(columns, axis=1))) * (spacing / length)
    for transfer in range(2):
        chosen = result[:, transfer * order : (transfer + 1) * order]
        pol_ref[transfer, 0] = chosen[slots:]
        pol_ref[transfer, 1] = -chosen[:slots]
    keep_ref[...] = pol_ref[mom_ref[0]]
    give_ref[...] = pol_ref[1 - mom_ref[0]]


def join_kernel(mom_ref, keep_ref, other_ref, out_ref):
    order = keep_ref.shape[2]
    first = mom_ref[0] == 0
    out_ref[0, :, :, :order] = jnp.where(first, keep_ref[...], other_ref[...])
    out_ref[0, :, :, order:] = jnp.where(first, other_ref[...], keep_ref[...])


def call(kernel, outs, scalars, name, scratch=()):
    vmem = pl.BlockSpec(memory_space=pltpu.VMEM)
    smem = pl.BlockSpec(memory_space=pltpu.SMEM)

    def run(*operands):
        return pl.pallas_call(
            kernel,
            out_shape=outs,
            in_specs=[smem] * scalars + [vmem] * (len(operands) - scalars),
            out_specs=jax.tree.map(lambda _: vmem, outs),
            scratch_shapes=list(scratch),
            name=name,
        )(*operands)

    return run


def exchange(chunks):
    return lax.all_to_all(chunks, ("energy", "mom"), split_axis=0, concat_axis=0, tiled=True)


def split_table(table):
    high = table.astype(np.float32).astype(jnp.bfloat16)
    low = (table - high.astype(np.float64)).astype(np.float32).astype(jnp.bfloat16)
    return np.stack([high, low])


def on_device(hamiltonian, hopping, self_energy, screened, energy_map):
    slots = lax.axis_size("energy")
    spacing = energy_span / slots
    length = 2 * slots
    order = hamiltonian.shape[-1]
    angle = (np.arange(length)[:, None] * np.arange(slots)[None, :] % length) * (
        2.0 * math.pi / length
    )
    wave = np.stack([np.cos(angle), -np.sin(angle)])
    wave_t = np.swapaxes(wave, 1, 2)
    back = np.block([[wave_t[0], wave_t[1]], [-wave_t[1], wave_t[0]]])
    wave, wave_t, back = (jnp.asarray(split_table(t)) for t in (wave, wave_t, back))

    def f32(*shape):
        return jax.ShapeDtypeStruct(shape, jnp.float32)

    def b16(*shape):
        return jax.ShapeDtypeStruct(shape, jnp.bfloat16)

    moment = lax.axis_index("mom").astype(jnp.int32).reshape(1)
    targets = 2 * slots
    column = lax.axis_index(("energy", "mom")).astype(jnp.int32).reshape(1) % order
    fields = call(
        lambda *refs: green_kernel(spacing, *refs), f32(targets * field_rows, order), 1, "green"
    )(energy_map, hamiltonian, hopping, self_energy, screened)
    own = exchange(fields.reshape(targets, field_rows, order)).reshape(fields.shape)
    send, forward, lesser_hat, occupied = call(
        lambda *refs: sigma_kernel(spacing, *refs),
        (
            f32(2 * targets, order),
            b16(2, 2 * length, 2 * slots),
            f32(2 * length, 2 * order),
            f32(slots, order),
        ),
        1,
        "sigma",
    )(column, own, wave, wave_t)
    returned = exchange(send.reshape(targets, 2, order))
    keep, give = call(
        lambda *refs: polar_kernel(spacing, *refs),
        (f32(2, slots, order), f32(2, slots, order)),
        2,
        "polar",
        [pltpu.VMEM((2, 2, slots, order), jnp.float32)],
    )(moment, column, own, occupied, forward, back, lesser_hat)
    other = from_partner(give, "mom")
    polar = call(join_kernel, f32(1, 2, slots, 2 * order), 1, "join")(moment, keep, other)
    new_sigma = jnp.swapaxes(returned, 0, 1).reshape(screened.shape)
    return (new_sigma, polar)


def solution(mesh):
    return jax.shard_map(
        on_device,
        mesh=mesh,
        in_specs=(
            P("mom", None, None, None, None),
            P("mom", None, None, None),
            P("mom", "energy", None, None, None, None),
            P("mom", "energy", None, None, None, None),
            P("energy"),
        ),
        out_specs=(P("mom", "energy", None, None, None, None), P("mom", None, None, "energy")),
        check_vma=False,
    )
```

```python
import math

import jax
import jax.numpy as jnp
import numpy as np
from jax import lax
from jax.experimental import pallas as pl
from jax.experimental.pallas import tpu as pltpu
from jax.sharding import PartitionSpec as P

energy_floor = -2.0
energy_span = 4.0
broadening = 1.0
chemical = 0.0
thermal = 0.25

field_rows = 4


def from_partner(array, axis):
    return lax.ppermute(array, axis, [(i, i ^ 1) for i in range(lax.axis_size(axis))])


def occupation(energy):
    return 1.0 / (1.0 + jnp.exp((energy - chemical) / thermal))


def halves(value):
    high = value.astype(jnp.bfloat16)
    return high, (value - high.astype(jnp.float32)).astype(jnp.bfloat16)


def dot(left, right):
    return jnp.dot(left, right, preferred_element_type=jnp.float32)


def dot3(left, right):
    return dot(left[0], right[0]) + (dot(left[0], right[1]) + dot(left[1], right[0]))


def left_form(pair):
    return halves(jnp.concatenate(pair, axis=1))


def right_form(pair):
    re, im = halves(pair[0]), halves(pair[1])
    return tuple(
        jnp.concatenate(
            [jnp.concatenate([re[n], im[n]], axis=1), jnp.concatenate([-im[n], re[n]], axis=1)],
            axis=0,
        )
        for n in range(2)
    )


def cproduct(left, right):
    result = dot3(left, right)
    order = result.shape[0]
    return result[:, :order], result[:, order:]


def approx_inverse(mat_re, mat_im, eye):
    def diagonal(values, axis):
        return jnp.sum(jnp.where(eye, values, 0.0), axis=axis, keepdims=True)

    def reciprocal(axis):
        diag_re, diag_im = diagonal(mat_re, axis), diagonal(mat_im, axis)
        magnitude = diag_re * diag_re + diag_im * diag_im
        return diag_re / magnitude, -diag_im / magnitude

    col_re, col_im = reciprocal(1)
    row_re, row_im = reciprocal(0)
    outer_re = col_re * row_re - col_im * row_im
    outer_im = col_re * row_im + col_im * row_re
    first_re = jnp.where(eye, 2.0 * row_re, 0.0) - (outer_re * mat_re - outer_im * mat_im)
    first_im = jnp.where(eye, 2.0 * row_im, 0.0) - (outer_re * mat_im + outer_im * mat_re)
    first = (first_re, first_im)
    applied = cproduct(left_form((mat_re, mat_im)), right_form(first))
    second = cproduct(left_form(first), right_form(applied))
    return 2.0 * first_re - second[0], 2.0 * first_im - second[1]


def green_kernel(spacing, map_ref, ham_ref, hop_ref, self_ref, screened_ref, out_ref):
    order = ham_ref.shape[3]
    rows = lax.broadcasted_iota(jnp.int32, (order, order), 0)
    cols = lax.broadcasted_iota(jnp.int32, (order, order), 1)
    eye = rows == cols
    index = jnp.full((order, order), map_ref[0], jnp.int32).astype(jnp.float32)
    energy = energy_floor + spacing * index

    def put(block, row, values):
        start = block * order * field_rows + row
        out_ref[pl.ds(start, order, stride=field_rows), :] = values

    def shifted(block):
        raw_re, raw_im = ham_ref[0, block, 0], ham_ref[0, block, 1]
        herm_re = 0.5 * (raw_re + raw_re.T)
        herm_im = 0.5 * (raw_im - raw_im.T)
        return (
            jnp.where(eye, energy, 0.0) - herm_re - self_ref[0, 0, 0, block],
            jnp.where(eye, broadening, 0.0) - herm_im - self_ref[0, 0, 1, block],
        )

    for block in range(2):
        put(block, 2, screened_ref[0, 0, 0, block])
        put(block, 3, screened_ref[0, 0, 1, block])
    hop = (hop_ref[0, 0], hop_ref[0, 1])
    adjoint = (hop[0].T, -hop[1].T)
    hop_right = right_form(hop)
    local = approx_inverse(*shifted(0), eye)
    incoming = cproduct(left_form(adjoint), right_form(local))
    outgoing = cproduct(left_form(local), hop_right)
    coupled = cproduct(left_form(incoming), hop_right)
    last = shifted(1)
    green = approx_inverse(last[0] - coupled[0], last[1] - coupled[1], eye)
    middle = cproduct(left_form(outgoing), right_form(green))
    middle = cproduct(left_form(middle), right_form(incoming))
    full = ((local[0] + middle[0], local[1] + middle[1]), green)
    for block in range(2):
        put(block, 0, -(full[block][1] + full[block][1].T))
        put(block, 1, jnp.where(eye, index, full[block][0] - full[block][0].T))


def rows_of(ref, moment, row):
    slots = ref.shape[0] // (2 * field_rows)
    return ref[pl.ds(moment * field_rows + row, slots, stride=2 * field_rows), :]


def on_diagonal(column_ref, shape):
    return lax.broadcasted_iota(jnp.int32, shape, 1) == column_ref[0]


def spectrum(ref, diagonal, scale):
    real = [scale * rows_of(ref, moment, 0) for moment in range(2)]
    imag = [
        jnp.where(diagonal, 0.0, scale * rows_of(ref, moment, 1)) for moment in range(2)
    ]
    return jnp.concatenate(
        [jnp.concatenate(real, axis=1), jnp.concatenate(imag, axis=1)], axis=0
    )


def interaction(ref):
    return jnp.concatenate(
        [
            jnp.concatenate([rows_of(ref, moment, row) for moment in range(2)], axis=1)
            for row in (2, 3)
        ],
        axis=0,
    )


def sigma_kernel(
    spacing, column_ref, recv_ref, wave_ref, wave_t_ref, send_ref, fwd_ref, hat_ref, occ_ref
):
    slots, order = occ_ref.shape
    length = 2 * slots
    diagonal = on_diagonal(column_ref, occ_ref.shape)
    index = jnp.sum(
        jnp.where(diagonal, rows_of(recv_ref, 0, 1), 0.0), axis=1, keepdims=True
    )
    index = jnp.broadcast_to(index, occ_ref.shape)
    occupied = occupation(energy_floor + spacing * index)
    occ_ref[...] = occupied
    grid = lax.broadcasted_iota(jnp.int32, index.shape, 1).astype(jnp.float32)
    chosen = jnp.where(index == grid, 1.0, 0.0).astype(jnp.bfloat16)
    contract = (((1,), (1,)), ((), ()))
    forward, inverse = [], []
    for n in range(2):
        wave = [
            lax.dot_general(
                wave_ref[n, part], chosen, contract, preferred_element_type=jnp.float32
            ).astype(jnp.bfloat16)
            for part in range(2)
        ]
        forward.append(
            jnp.concatenate(
                [
                    jnp.concatenate([wave[0], -wave[1]], axis=1),
                    jnp.concatenate([wave[1], wave[0]], axis=1),
                ],
                axis=0,
            )
        )
        fwd_ref[n] = forward[n]
        turned = [dot(chosen, wave_t_ref[n, part]).astype(jnp.bfloat16) for part in range(2)]
        inverse.append(
            jnp.concatenate(
                [
                    jnp.concatenate([turned[0], turned[1]], axis=1),
                    jnp.concatenate([-turned[1], turned[0]], axis=1),
                ],
                axis=0,
            )
        )
    lesser = dot3(forward, halves(spectrum(recv_ref, diagonal, occupied)))
    inter = dot3(forward, halves(interaction(recv_ref)))
    hat_ref[...] = lesser

    def parts(hat, moment):
        return (
            hat[:length, moment * order : (moment + 1) * order],
            hat[length:, moment * order : (moment + 1) * order],
        )

    columns = []
    for moment in range(2):
        sum_re = sum_im = 0.0
        for transfer in range(2):
            left_re, left_im = parts(lesser, (moment - transfer) % 2)
            right_re, right_im = parts(inter, transfer)
            sum_re += left_re * right_re - left_im * right_im
            sum_im += left_re * right_im + left_im * right_re
        columns.append(jnp.concatenate([sum_re, sum_im], axis=0))
    result = dot3(inverse, halves(jnp.concatenate(columns, axis=1))) * (-spacing / length)
    for moment in range(2):
        for part in range(2):
            send_ref[pl.ds(moment * 2 + part, slots, stride=4), :] = result[
                part * slots : (part + 1) * slots, moment * order : (moment + 1) * order
            ]


def polar_kernel(
    spacing,
    mom_ref,
    column_ref,
    recv_ref,
    occ_ref,
    fwd_ref,
    back_ref,
    hat_ref,
    keep_ref,
    give_ref,
    pol_ref,
):
    slots, order = occ_ref.shape
    length = 2 * slots
    forward = (fwd_ref[0], fwd_ref[1])
    diagonal = on_diagonal(column_ref, occ_ref.shape)
    greater = dot3(forward, halves(spectrum(recv_ref, diagonal, 1.0 - occ_ref[...])))

    def parts(hat, moment):
        return (
            hat[:length, moment * order : (moment + 1) * order],
            hat[length:, moment * order : (moment + 1) * order],
        )

    columns = []
    for transfer in range(2):
        sum_re = sum_im = 0.0
        for moment in range(2):
            left_re, left_im = parts(greater, moment)
            right_re, right_im = parts(hat_ref, (moment - transfer) % 2)
            sum_re += left_re * right_re + left_im * right_im
            sum_im += left_im * right_re - left_re * right_im
        columns.append(jnp.concatenate([sum_re, sum_im], axis=0))
    back = (back_ref[0], back_ref[1])
    result = dot3(back, halves(jnp.concatenate(columns, axis=1))) * (spacing / length)
    for transfer in range(2):
        chosen = result[:, transfer * order : (transfer + 1) * order]
        pol_ref[transfer, 0] = chosen[slots:]
        pol_ref[transfer, 1] = -chosen[:slots]
    keep_ref[...] = pol_ref[mom_ref[0]]
    give_ref[...] = pol_ref[1 - mom_ref[0]]


def join_kernel(mom_ref, keep_ref, other_ref, out_ref):
    order = keep_ref.shape[2]
    first = mom_ref[0] == 0
    out_ref[0, :, :, :order] = jnp.where(first, keep_ref[...], other_ref[...])
    out_ref[0, :, :, order:] = jnp.where(first, other_ref[...], keep_ref[...])


def call(kernel, outs, scalars, name, scratch=()):
    vmem = pl.BlockSpec(memory_space=pltpu.VMEM)
    smem = pl.BlockSpec(memory_space=pltpu.SMEM)

    def run(*operands):
        return pl.pallas_call(
            kernel,
            out_shape=outs,
            in_specs=[smem] * scalars + [vmem] * (len(operands) - scalars),
            out_specs=jax.tree.map(lambda _: vmem, outs),
            scratch_shapes=list(scratch),
            name=name,
        )(*operands)

    return run


def resident(array):
    return pltpu.with_memory_space_constraint(array, pltpu.VMEM)


def exchange(chunks):
    return lax.all_to_all(chunks, ("energy", "mom"), split_axis=0, concat_axis=0, tiled=True)


def split_table(table):
    high = table.astype(np.float32).astype(jnp.bfloat16)
    low = (table - high.astype(np.float64)).astype(np.float32).astype(jnp.bfloat16)
    return np.stack([high, low])


def on_device(hamiltonian, hopping, self_energy, screened, energy_map):
    slots = lax.axis_size("energy")
    spacing = energy_span / slots
    length = 2 * slots
    order = hamiltonian.shape[-1]
    angle = (np.arange(length)[:, None] * np.arange(slots)[None, :] % length) * (
        2.0 * math.pi / length
    )
    wave = np.stack([np.cos(angle), -np.sin(angle)])
    wave_t = np.swapaxes(wave, 1, 2)
    back = np.block([[wave_t[0], wave_t[1]], [-wave_t[1], wave_t[0]]])
    wave, wave_t, back = (jnp.asarray(split_table(t)) for t in (wave, wave_t, back))

    def f32(*shape):
        return jax.ShapeDtypeStruct(shape, jnp.float32)

    moment = lax.axis_index("mom").astype(jnp.int32).reshape(1)
    def held(*shape, kind=jnp.float32):
        return pltpu.VMEM(shape, kind)

    targets = 2 * slots
    column = lax.axis_index(("energy", "mom")).astype(jnp.int32).reshape(1) % order
    fields = call(
        lambda *refs: green_kernel(spacing, *refs), f32(targets * field_rows, order), 1, "green"
    )(energy_map, hamiltonian, hopping, self_energy, screened)
    own = resident(exchange(fields.reshape(targets, field_rows, order)).reshape(fields.shape))
    send, forward, lesser_hat, occupied = call(
        lambda *refs: sigma_kernel(spacing, *refs),
        (
            f32(2 * targets, order),
            held(2, 2 * length, 2 * slots, kind=jnp.bfloat16),
            held(2 * length, 2 * order),
            held(slots, order),
        ),
        1,
        "sigma",
    )(column, own, resident(wave), resident(wave_t))
    returned = exchange(send.reshape(targets, 2, order))
    keep, give = call(
        lambda *refs: polar_kernel(spacing, *refs),
        (held(2, slots, order), held(2, slots, order)),
        2,
        "polar",
        [pltpu.VMEM((2, 2, slots, order), jnp.float32)],
    )(
        moment,
        column,
        own,
        resident(occupied),
        resident(forward),
        resident(back),
        resident(lesser_hat),
    )
    other = resident(from_partner(give, "mom"))
    polar = call(join_kernel, f32(1, 2, slots, 2 * order), 1, "join")(
        moment, resident(keep), other
    )
    new_sigma = jnp.swapaxes(returned, 0, 1).reshape(screened.shape)
    return (new_sigma, polar)


def solution(mesh):
    return jax.shard_map(
        on_device,
        mesh=mesh,
        in_specs=(
            P("mom", None, None, None, None),
            P("mom", None, None, None),
            P("mom", "energy", None, None, None, None),
            P("mom", "energy", None, None, None, None),
            P("energy"),
        ),
        out_specs=(P("mom", "energy", None, None, None, None), P("mom", None, None, "energy")),
        check_vma=False,
    )
```

```python
import math

import jax
import jax.numpy as jnp
import numpy as np
from jax import lax
from jax.experimental import pallas as pl
from jax.experimental.pallas import tpu as pltpu
from jax.sharding import PartitionSpec as P

energy_floor = -2.0
energy_span = 4.0
broadening = 1.0
chemical = 0.0
thermal = 0.25

field_rows = 4


def from_partner(array, axis):
    return lax.ppermute(array, axis, [(i, i ^ 1) for i in range(lax.axis_size(axis))])


def occupation(energy):
    return 1.0 / (1.0 + jnp.exp((energy - chemical) / thermal))


def halves(value):
    high = value.astype(jnp.bfloat16)
    return high, (value - high.astype(jnp.float32)).astype(jnp.bfloat16)


def dot(left, right):
    return jnp.dot(left, right, preferred_element_type=jnp.float32)


def dot3(left, right):
    rows = left[0].shape[0]
    both = dot(jnp.concatenate(left, axis=0), right[0])
    return both[:rows] + (dot(left[0], right[1]) + both[rows:])


def left_form(pair):
    return halves(jnp.concatenate(pair, axis=1))


def right_form(pair):
    re, im = halves(pair[0]), halves(pair[1])
    return tuple(
        jnp.concatenate(
            [jnp.concatenate([re[n], im[n]], axis=1), jnp.concatenate([-im[n], re[n]], axis=1)],
            axis=0,
        )
        for n in range(2)
    )


def cproduct(left, right):
    order = left[0].shape[0]
    result = dot(
        jnp.concatenate([left[0], left[0], left[1]], axis=1),
        jnp.concatenate([right[0], right[1], right[0]], axis=0),
    )
    return result[:, :order], result[:, order:]


def approx_inverse(mat_re, mat_im, eye):
    def diagonal(values, axis):
        return jnp.sum(jnp.where(eye, values, 0.0), axis=axis, keepdims=True)

    def reciprocal(axis):
        diag_re, diag_im = diagonal(mat_re, axis), diagonal(mat_im, axis)
        magnitude = diag_re * diag_re + diag_im * diag_im
        return diag_re / magnitude, -diag_im / magnitude

    col_re, col_im = reciprocal(1)
    row_re, row_im = reciprocal(0)
    outer_re = col_re * row_re - col_im * row_im
    outer_im = col_re * row_im + col_im * row_re
    first_re = jnp.where(eye, 2.0 * row_re, 0.0) - (outer_re * mat_re - outer_im * mat_im)
    first_im = jnp.where(eye, 2.0 * row_im, 0.0) - (outer_re * mat_im + outer_im * mat_re)
    first = (first_re, first_im)
    applied = cproduct(left_form((mat_re, mat_im)), right_form(first))
    second = cproduct(left_form(first), right_form(applied))
    return 2.0 * first_re - second[0], 2.0 * first_im - second[1]


def green_kernel(
    spacing,
    map_ref,
    ham_hbm,
    hop_hbm,
    self_hbm,
    screened_hbm,
    out_ref,
    ham_ref,
    hop_ref,
    self_ref,
    screened_ref,
    semaphores,
):
    copies = [
        pltpu.make_async_copy(source, target, semaphores.at[n])
        for n, (source, target) in enumerate(
            (
                (ham_hbm, ham_ref),
                (self_hbm, self_ref),
                (hop_hbm, hop_ref),
                (screened_hbm, screened_ref),
            )
        )
    ]
    for copy in copies:
        copy.start()
    order = ham_ref.shape[3]
    rows = lax.broadcasted_iota(jnp.int32, (order, order), 0)
    cols = lax.broadcasted_iota(jnp.int32, (order, order), 1)
    eye = rows == cols
    index = jnp.full((order, order), map_ref[0], jnp.int32).astype(jnp.float32)
    energy = energy_floor + spacing * index

    def put(block, row, values):
        start = block * order * field_rows + row
        out_ref[pl.ds(start, order, stride=field_rows), :] = values

    def shifted(block):
        raw_re, raw_im = ham_ref[0, block, 0], ham_ref[0, block, 1]
        herm_re = 0.5 * (raw_re + raw_re.T)
        herm_im = 0.5 * (raw_im - raw_im.T)
        return (
            jnp.where(eye, energy, 0.0) - herm_re - self_ref[0, 0, 0, block],
            jnp.where(eye, broadening, 0.0) - herm_im - self_ref[0, 0, 1, block],
        )

    copies[0].wait()
    copies[1].wait()
    local = approx_inverse(*shifted(0), eye)
    last = shifted(1)
    copies[2].wait()
    copies[3].wait()
    for block in range(2):
        put(block, 2, screened_ref[0, 0, 0, block])
        put(block, 3, screened_ref[0, 0, 1, block])
    hop = (hop_ref[0, 0], hop_ref[0, 1])
    adjoint = (hop[0].T, -hop[1].T)
    hop_right = right_form(hop)
    incoming = cproduct(left_form(adjoint), right_form(local))
    outgoing = cproduct(left_form(local), hop_right)
    coupled = cproduct(left_form(incoming), hop_right)
    green = approx_inverse(last[0] - coupled[0], last[1] - coupled[1], eye)
    middle = cproduct(left_form(outgoing), right_form(green))
    middle = cproduct(left_form(middle), right_form(incoming))
    full = ((local[0] + middle[0], local[1] + middle[1]), green)
    for block in range(2):
        put(block, 0, -(full[block][1] + full[block][1].T))
        put(block, 1, jnp.where(eye, index, full[block][0] - full[block][0].T))


def rows_of(ref, moment, row):
    slots = ref.shape[0] // (2 * field_rows)
    return ref[pl.ds(moment * field_rows + row, slots, stride=2 * field_rows), :]


def on_diagonal(column_ref, shape):
    return lax.broadcasted_iota(jnp.int32, shape, 1) == column_ref[0]


def spectrum(ref, diagonal, scale):
    real = [scale * rows_of(ref, moment, 0) for moment in range(2)]
    imag = [
        jnp.where(diagonal, 0.0, scale * rows_of(ref, moment, 1)) for moment in range(2)
    ]
    return jnp.concatenate(
        [jnp.concatenate(real, axis=1), jnp.concatenate(imag, axis=1)], axis=0
    )


def interaction(ref):
    return jnp.concatenate(
        [
            jnp.concatenate([rows_of(ref, moment, row) for moment in range(2)], axis=1)
            for row in (2, 3)
        ],
        axis=0,
    )


def sigma_kernel(
    spacing, column_ref, recv_ref, wave_ref, wave_t_ref, send_ref, fwd_ref, hat_ref, occ_ref
):
    slots, order = occ_ref.shape
    length = 2 * slots
    diagonal = on_diagonal(column_ref, occ_ref.shape)
    index = jnp.sum(
        jnp.where(diagonal, rows_of(recv_ref, 0, 1), 0.0), axis=1, keepdims=True
    )
    index = jnp.broadcast_to(index, occ_ref.shape)
    occupied = occupation(energy_floor + spacing * index)
    occ_ref[...] = occupied
    grid = lax.broadcasted_iota(jnp.int32, index.shape, 1).astype(jnp.float32)
    chosen = jnp.where(index == grid, 1.0, 0.0).astype(jnp.bfloat16)
    contract = (((1,), (1,)), ((), ()))
    forward, inverse = [], []
    for n in range(2):
        wave = [
            lax.dot_general(
                wave_ref[n, part], chosen, contract, preferred_element_type=jnp.float32
            ).astype(jnp.bfloat16)
            for part in range(2)
        ]
        forward.append(
            jnp.concatenate(
                [
                    jnp.concatenate([wave[0], -wave[1]], axis=1),
                    jnp.concatenate([wave[1], wave[0]], axis=1),
                ],
                axis=0,
            )
        )
        fwd_ref[n] = forward[n]
        turned = [dot(chosen, wave_t_ref[n, part]).astype(jnp.bfloat16) for part in range(2)]
        inverse.append(
            jnp.concatenate(
                [
                    jnp.concatenate([turned[0], turned[1]], axis=1),
                    jnp.concatenate([-turned[1], turned[0]], axis=1),
                ],
                axis=0,
            )
        )
    lesser = dot3(forward, halves(spectrum(recv_ref, diagonal, occupied)))
    inter = dot3(forward, halves(interaction(recv_ref)))
    hat_ref[...] = lesser

    def parts(hat, moment):
        return (
            hat[:length, moment * order : (moment + 1) * order],
            hat[length:, moment * order : (moment + 1) * order],
        )

    columns = []
    for moment in range(2):
        sum_re = sum_im = 0.0
        for transfer in range(2):
            left_re, left_im = parts(lesser, (moment - transfer) % 2)
            right_re, right_im = parts(inter, transfer)
            sum_re += left_re * right_re - left_im * right_im
            sum_im += left_re * right_im + left_im * right_re
        columns.append(jnp.concatenate([sum_re, sum_im], axis=0))
    result = dot3(inverse, halves(jnp.concatenate(columns, axis=1))) * (-spacing / length)
    for moment in range(2):
        for part in range(2):
            send_ref[pl.ds(moment * 2 + part, slots, stride=4), :] = result[
                part * slots : (part + 1) * slots, moment * order : (moment + 1) * order
            ]


def polar_kernel(
    spacing,
    mom_ref,
    column_ref,
    recv_ref,
    occ_ref,
    fwd_ref,
    back_ref,
    hat_ref,
    keep_ref,
    give_ref,
    pol_ref,
):
    slots, order = occ_ref.shape
    length = 2 * slots
    forward = (fwd_ref[0], fwd_ref[1])
    diagonal = on_diagonal(column_ref, occ_ref.shape)
    greater = dot3(forward, halves(spectrum(recv_ref, diagonal, 1.0 - occ_ref[...])))

    def parts(hat, moment):
        return (
            hat[:length, moment * order : (moment + 1) * order],
            hat[length:, moment * order : (moment + 1) * order],
        )

    columns = []
    for transfer in range(2):
        sum_re = sum_im = 0.0
        for moment in range(2):
            left_re, left_im = parts(greater, moment)
            right_re, right_im = parts(hat_ref, (moment - transfer) % 2)
            sum_re += left_re * right_re + left_im * right_im
            sum_im += left_im * right_re - left_re * right_im
        columns.append(jnp.concatenate([sum_re, sum_im], axis=0))
    back = (back_ref[0], back_ref[1])
    result = dot3(back, halves(jnp.concatenate(columns, axis=1))) * (spacing / length)
    for transfer in range(2):
        chosen = result[:, transfer * order : (transfer + 1) * order]
        pol_ref[transfer, 0] = chosen[slots:]
        pol_ref[transfer, 1] = -chosen[:slots]
    keep_ref[...] = pol_ref[mom_ref[0]]
    give_ref[...] = pol_ref[1 - mom_ref[0]]


def join_kernel(mom_ref, keep_ref, other_ref, out_ref):
    order = keep_ref.shape[2]
    first = mom_ref[0] == 0
    out_ref[0, :, :, :order] = jnp.where(first, keep_ref[...], other_ref[...])
    out_ref[0, :, :, order:] = jnp.where(first, other_ref[...], keep_ref[...])


def call(kernel, outs, scalars, name, scratch=(), hbm=False):
    vmem = pl.BlockSpec(memory_space=pltpu.VMEM)
    smem = pl.BlockSpec(memory_space=pltpu.SMEM)

    source = pl.BlockSpec(memory_space=pltpu.HBM) if hbm else vmem

    def run(*operands):
        return pl.pallas_call(
            kernel,
            out_shape=outs,
            in_specs=[smem] * scalars + [source] * (len(operands) - scalars),
            out_specs=jax.tree.map(lambda _: vmem, outs),
            scratch_shapes=list(scratch),
            name=name,
        )(*operands)

    return run


def resident(array):
    return pltpu.with_memory_space_constraint(array, pltpu.VMEM)


def exchange(chunks):
    return lax.all_to_all(chunks, ("energy", "mom"), split_axis=0, concat_axis=0, tiled=True)


def split_table(table):
    high = table.astype(np.float32).astype(jnp.bfloat16)
    low = (table - high.astype(np.float64)).astype(np.float32).astype(jnp.bfloat16)
    return np.stack([high, low])


def on_device(hamiltonian, hopping, self_energy, screened, energy_map):
    slots = lax.axis_size("energy")
    spacing = energy_span / slots
    length = 2 * slots
    order = hamiltonian.shape[-1]
    angle = (np.arange(length)[:, None] * np.arange(slots)[None, :] % length) * (
        2.0 * math.pi / length
    )
    wave = np.stack([np.cos(angle), -np.sin(angle)])
    wave_t = np.swapaxes(wave, 1, 2)
    back = np.block([[wave_t[0], wave_t[1]], [-wave_t[1], wave_t[0]]])
    wave, wave_t, back = (jnp.asarray(split_table(t)) for t in (wave, wave_t, back))

    def f32(*shape):
        return jax.ShapeDtypeStruct(shape, jnp.float32)

    moment = lax.axis_index("mom").astype(jnp.int32).reshape(1)
    def held(*shape, kind=jnp.float32):
        return pltpu.VMEM(shape, kind)

    targets = 2 * slots
    column = lax.axis_index(("energy", "mom")).astype(jnp.int32).reshape(1) % order
    sources = (hamiltonian, hopping, self_energy, screened)
    fields = call(
        lambda *refs: green_kernel(spacing, *refs), f32(targets * field_rows, order), 1, "green",
        [pltpu.VMEM(array.shape, jnp.float32) for array in sources]
        + [pltpu.SemaphoreType.DMA((4,))],
        hbm=True,
    )(energy_map, *sources)
    own = resident(exchange(fields.reshape(targets, field_rows, order)).reshape(fields.shape))
    send, forward, lesser_hat, occupied = call(
        lambda *refs: sigma_kernel(spacing, *refs),
        (
            f32(2 * targets, order),
            held(2, 2 * length, 2 * slots, kind=jnp.bfloat16),
            held(2 * length, 2 * order),
            held(slots, order),
        ),
        1,
        "sigma",
    )(column, own, resident(wave), resident(wave_t))
    returned = exchange(send.reshape(targets, 2, order))
    keep, give = call(
        lambda *refs: polar_kernel(spacing, *refs),
        (held(2, slots, order), held(2, slots, order)),
        2,
        "polar",
        [pltpu.VMEM((2, 2, slots, order), jnp.float32)],
    )(
        moment,
        column,
        own,
        resident(occupied),
        resident(forward),
        resident(back),
        resident(lesser_hat),
    )
    other = resident(from_partner(give, "mom"))
    polar = call(join_kernel, f32(1, 2, slots, 2 * order), 1, "join")(
        moment, resident(keep), other
    )
    new_sigma = jnp.swapaxes(returned, 0, 1).reshape(screened.shape)
    return (new_sigma, polar)


def solution(mesh):
    return jax.shard_map(
        on_device,
        mesh=mesh,
        in_specs=(
            P("mom", None, None, None, None),
            P("mom", None, None, None),
            P("mom", "energy", None, None, None, None),
            P("mom", "energy", None, None, None, None),
            P("energy"),
        ),
        out_specs=(P("mom", "energy", None, None, None, None), P("mom", None, None, "energy")),
        check_vma=False,
    )
```
